32 devices in a mesh: dp: 4 (over x, core), fsdp: 8 (over z, y).
Axes of the slice: x: 2, y: 2, z: 4, core: 2. Of those that a mesh axis runs over, the one named last changes fastest.
Arguments:
- token_ids: int32 [32, 128], P(('dp', 'fsdp')), may hold values from 0 to 50431
- seq_lengths: int32 [32], P(('dp', 'fsdp')), may hold values from 32 to 128, as said below
- pair_margins: int32 [16], replicated, may hold values from 1 to 3
- pair_valid: int32 [16], replicated, may hold values from 0 to 1, as said below
- embed_table: bfloat16 [50432, 512], P('fsdp'), may hold values from -6 to 6
- in_proj: bfloat16 [512, 1536], P('fsdp'), may hold values from -0.375 to 0.375
- out_proj: bfloat16 [512, 512], P('fsdp'), may hold values from -0.5 to 0.5
- up_proj: bfloat16 [512, 2048], P('fsdp'), may hold values from -0.25 to 0.25
- down_proj: bfloat16 [2048, 512], P('fsdp'), may hold values from -0.125 to 0.125
- small_params: bfloat16 [7680], replicated, may hold values from -0.5 to 1.75, as said below
- reward_heads: bfloat16 [512, 8], replicated, may hold values from -0.25 to 0.25
- first_embed: bfloat16 [50432, 512], P('fsdp'), may hold values from -0.00061035156 to 0.00061035156
- first_in: bfloat16 [512, 1536], P('fsdp'), may hold values from -0.00390625 to 0.00390625
- first_out: bfloat16 [512, 512], P('fsdp'), may hold values from -0.00390625 to 0.00390625
- first_up: bfloat16 [512, 2048], P('fsdp'), may hold values from -0.00390625 to 0.00390625
- first_down: bfloat16 [2048, 512], P('fsdp'), may hold values from -0.00390625 to 0.00390625
- first_small: bfloat16 [7680], replicated, may hold values from -0.00390625 to 0.00390625
- first_heads: bfloat16 [512, 8], replicated, may hold values from -0.01953125 to 0.01953125
- second_embed: bfloat16 [50432, 512], P('fsdp'), may hold values from 9.531504e-10 to 3.812602e-09
- second_in: bfloat16 [512, 1536], P('fsdp'), may hold values from 3.0500814e-08 to 1.2200326e-07
- second_out: bfloat16 [512, 512], P('fsdp'), may hold values from 3.0500814e-08 to 1.2200326e-07
- second_up: bfloat16 [512, 2048], P('fsdp'), may hold values from 3.0500814e-08 to 1.2200326e-07
- second_down: bfloat16 [2048, 512], P('fsdp'), may hold values from 3.0500814e-08 to 1.2200326e-07
- second_small: bfloat16 [7680], replicated, may hold values from 3.0500814e-08 to 1.2200326e-07
- second_heads: bfloat16 [512, 8], replicated, may hold values from 9.760261e-07 to 3.9041042e-06
Outputs:
- loss: float32 [], replicated
- norms: float32 [2, 7], replicated
- embed_new: float32 [50432, 512], P('fsdp')
- embed_first: float32 [50432, 512], P('fsdp')
- embed_second: float32 [50432, 512], P('fsdp')
- in_new: float32 [512, 1536], P('fsdp')
- in_first: float32 [512, 1536], P('fsdp')
- in_second: float32 [512, 1536], P('fsdp')
- out_new: float32 [512, 512], P('fsdp')
- out_first: float32 [512, 512], P('fsdp')
- out_second: float32 [512, 512], P('fsdp')
- up_new: float32 [512, 2048], P('fsdp')
- up_first: float32 [512, 2048], P('fsdp')
- up_second: float32 [512, 2048], P('fsdp')
- down_new: float32 [2048, 512], P('fsdp')
- down_first: float32 [2048, 512], P('fsdp')
- down_second: float32 [2048, 512], P('fsdp')
- small_new: float32 [7680], replicated
- small_first: float32 [7680], replicated
- small_second: float32 [7680], replicated
- heads_new: float32 [512, 8], replicated
- heads_first: float32 [512, 8], replicated
- heads_second: float32 [512, 8], replicated
The draws below stay inside these ranges and needn't reach their ends.
Inputs may be any that keep to these rules, and one draw needn't show every extreme that they name: `seq_lengths`: each sequence counts between a quarter of 128 and 128 tokens; the first counts 128, the second a quarter of 128; later slots are padding. `pair_valid`: the first pair counts and the second does not. `small_params`: gains near 1, biases near 0.
All inputs are finite; a program needn't handle non-finite values.
Results may differ from the reference program's by a relative error of at most 0.0068.
Values may be sent and summed in bfloat16 or wider, within the bound.
No kernel may reach another device: no remote copies, remote signals or barrier semaphores. Data moves between devices by JAX's collectives and lax.ppermute only.
A program may use at most 192 MiB of HBM per device.

```python
import math
import jax
import jax.numpy as jnp
import numpy as np
from jax import lax

D = 512
HEADS = 8
HEAD = 64
ROT = 16
FF = 2048
V = 50432
K = 8
STEP = 5
LEN = 128
SEQS = 32
PAIRS = 16
SMALL = 7680


def draw_seq_lengths(key, part):
    values = jax.random.randint(key, (SEQS,), LEN // 4, LEN + 1)
    return values.at[0].set(LEN).at[1].set(LEN // 4).astype(jnp.int32)


def draw_pair_valid(key, part):
    picks = jax.random.randint(key, (PAIRS,), 0, 4)
    return jnp.where(picks > 0, 1, 0).at[0].set(1).at[1].set(0).astype(jnp.int32)


def draw_small_params(key, part):
    index = jnp.arange(SMALL)
    noise = jnp.clip(jax.random.normal(key, (SMALL,), jnp.float32), -5.0, 5.0)
    gain_part = (index < 6 * D) & (index // D % 2 == 0)
    return jnp.where(gain_part, 1.0 + 0.15 * noise, 0.1 * noise).astype(jnp.bfloat16)


def plant(array, key, smallest, largest):
    index_at = [jax.random.randint(jax.random.fold_in(key, axis), (), 0, length) for axis, length in enumerate(array.shape)]
    main_axis = array.shape.index(max(array.shape))
    next_to = index_at[:main_axis] + [(index_at[main_axis] + 1) % array.shape[main_axis]] + index_at[main_axis + 1:]
    return array.at[tuple(index_at)].set(smallest).at[tuple(next_to)].set(largest)


def level_of(own_key, shape, cuts, low, largest):
    def one(axis_at, blocks):
        draws = jax.random.uniform(jax.random.fold_in(jax.random.fold_in(own_key, 6), axis_at), (blocks,), jnp.float32, low / len(cuts), largest / len(cuts))
        return jnp.repeat(jnp.exp(draws), shape[axis_at] // blocks).reshape((-1,) + (1,) * (len(shape) - axis_at - 1))

    loudness = one(*cuts[0])
    for cut in cuts[1:]:
        loudness = loudness * one(*cut)
    return loudness


def rank_bounds(number_of, skew):
    portions = [(1 << 20) // math.isqrt(standing ** skew) + 1 for standing in range(1, number_of + 1)]
    width = 1 + sum(portions) // (1 << 30)
    return np.cumsum(np.array([max(1, weight // width) for weight in portions]))


def ranked(stream_key, shape, count, slope):
    table = rank_bounds(count, slope)
    ticket = jax.random.randint(jax.random.fold_in(stream_key, 1), shape, 0, int(table[count - 1]))
    standing = jnp.searchsorted(jnp.asarray(table, jnp.int32), ticket, side="right")
    return jax.random.permutation(jax.random.fold_in(stream_key, 2), count)[standing].astype(jnp.int32)


def scatter_about(stream_key, shape, deviation, limit, shards=(), kind=jnp.bfloat16):
    values = deviation * jax.random.normal(stream_key, shape, jnp.float32)
    if shards:
        values = values * level_of(stream_key, shape, shards, -0.22, 0.18)
    return jnp.clip(values, -limit, limit).astype(kind)


def setup_inputs(seed: int = 0) -> dict:
    arg_keys = jax.random.split(jax.random.key(seed), 26)
    token_ids = plant(ranked(arg_keys[0], (SEQS, LEN), V, 2), jax.random.fold_in(arg_keys[0], 3), 0, V - 1).astype(jnp.int32)
    seq_lengths = draw_seq_lengths(jax.random.fold_in(arg_keys[25], 71), 0)
    pair_margins = plant(jax.random.randint(arg_keys[2], (PAIRS,), 1, 4), jax.random.fold_in(arg_keys[2], 1), 1, 3).astype(jnp.int32)
    pair_valid = draw_pair_valid(jax.random.fold_in(arg_keys[25], 71), 0)
    embed_table = scatter_about(arg_keys[4], (V, D), 1.0, 6.0, ((0, 8),))
    in_proj = scatter_about(arg_keys[5], (D, 3 * D), (D // 2) ** -0.5, 0.375, ((0, 8),))
    out_proj = scatter_about(arg_keys[6], (D, D), (D * 32 // LEN) ** -0.5, 0.5, ((0, 8),))
    up_proj = scatter_about(arg_keys[7], (D, FF), D ** -0.5, 0.25, ((0, 8),))
    down_proj = scatter_about(arg_keys[8], (FF, D), FF ** -0.5, 0.125, ((0, 8),))
    small_params = draw_small_params(jax.random.fold_in(arg_keys[25], 71), 0)
    reward_heads = scatter_about(arg_keys[10], (D, K), D ** -0.5, 0.25)
    first_embed = scatter_about(arg_keys[11], (V, D), (0.11 / (K ** 0.5 * PAIRS * D ** 0.5)), 0.00061035156, ((0, 8),))
    first_in = scatter_about(arg_keys[12], (D, 3 * D), (0.16 / (K * PAIRS * D) ** 0.5), 0.00390625, ((0, 8),))
    first_out = scatter_about(arg_keys[13], (D, D), (0.16 / (K * PAIRS * D) ** 0.5), 0.00390625, ((0, 8),))
    first_up = scatter_about(arg_keys[14], (D, FF), (0.16 / (K * PAIRS * D) ** 0.5), 0.00390625, ((0, 8),))
    first_down = scatter_about(arg_keys[15], (FF, D), (0.16 / (K * PAIRS * D) ** 0.5), 0.00390625, ((0, 8),))
    first_small = scatter_about(arg_keys[16], (SMALL,), (0.16 / (K * PAIRS * D) ** 0.5), 0.00390625)
    first_heads = scatter_about(arg_keys[17], (D, K), (0.11 / (K * PAIRS ** 0.5)), 0.01953125)
    second_embed = jnp.clip(jnp.exp(math.log(3.812601789832115e-09) - 1.3862944 * jax.random.uniform(arg_keys[18], (V, D), jnp.float32) ** level_of(arg_keys[18], (V, D), ((0, 8),), -0.2, 0.2)), 9.531504474580288e-10, 3.812601789832115e-09).astype(jnp.bfloat16)
    second_in = jnp.clip(jnp.exp(math.log(1.2200325727462769e-07) - 1.3862944 * jax.random.uniform(arg_keys[19], (D, 3 * D), jnp.float32) ** level_of(arg_keys[19], (D, 3 * D), ((0, 8),), -0.2, 0.2)), 3.050081431865692e-08, 1.2200325727462769e-07).astype(jnp.bfloat16)
    second_out = jnp.clip(jnp.exp(math.log(1.2200325727462769e-07) - 1.3862944 * jax.random.uniform(arg_keys[20], (D, D), jnp.float32) ** level_of(arg_keys[20], (D, D), ((0, 8),), -0.2, 0.2)), 3.050081431865692e-08, 1.2200325727462769e-07).astype(jnp.bfloat16)
    second_up = jnp.clip(jnp.exp(math.log(1.2200325727462769e-07) - 1.3862944 * jax.random.uniform(arg_keys[21], (D, FF), jnp.float32) ** level_of(arg_keys[21], (D, FF), ((0, 8),), -0.2, 0.2)), 3.050081431865692e-08, 1.2200325727462769e-07).astype(jnp.bfloat16)
    second_down = jnp.clip(jnp.exp(math.log(1.2200325727462769e-07) - 1.3862944 * jax.random.uniform(arg_keys[22], (FF, D), jnp.float32) ** level_of(arg_keys[22], (FF, D), ((0, 8),), -0.2, 0.2)), 3.050081431865692e-08, 1.2200325727462769e-07).astype(jnp.bfloat16)
    second_small = jnp.clip(jnp.exp(jax.random.uniform(arg_keys[23], (SMALL,), jnp.float32, math.log(3.050081431865692e-08), math.log(1.2200325727462769e-07))), 3.050081431865692e-08, 1.2200325727462769e-07).astype(jnp.bfloat16)
    second_heads = jnp.clip(jnp.exp(jax.random.uniform(arg_keys[24], (D, K), jnp.float32, math.log(9.760260581970215e-07), math.log(3.904104232788086e-06))), 9.760260581970215e-07, 3.904104232788086e-06).astype(jnp.bfloat16)
    return {"token_ids": token_ids, "seq_lengths": seq_lengths, "pair_margins": pair_margins, "pair_valid": pair_valid, "embed_table": embed_table, "in_proj": in_proj, "out_proj": out_proj, "up_proj": up_proj, "down_proj": down_proj, "small_params": small_params, "reward_heads": reward_heads, "first_embed": first_embed, "first_in": first_in, "first_out": first_out, "first_up": first_up, "first_down": first_down, "first_small": first_small, "first_heads": first_heads, "second_embed": second_embed, "second_in": second_in, "second_out": second_out, "second_up": second_up, "second_down": second_down, "second_small": second_small, "second_heads": second_heads}


@jax.custom_vjp
def low(v):
    return lax.optimization_barrier(v.astype(jnp.bfloat16)).astype(jnp.float32)

@jax.custom_vjp
def low_back(v):
    return v

def low_keep(v):
    return (low(v), None)

def low_pass(kept, grad):
    return (grad,)

def back_keep(v):
    return (v, None)

def back_low(kept, grad):
    return (low(grad),)
low.defvjp(low_keep, low_pass)
low_back.defvjp(back_keep, back_low)
norm_epsilon = 1e-05
beta_first = 0.9
beta_second = 0.999
adam_epsilon = 1e-06
weight_decay = 0.01
learn_rate = 0.3
rotary_base = 10000.0

def layer_norm(inputs, gain, shift):
    center = inputs - lax.optimization_barrier(jnp.mean(inputs, axis=-1, keepdims=True))
    spread = lax.optimization_barrier(jnp.mean(center * center, axis=-1, keepdims=True))
    return center * lax.rsqrt(spread + norm_epsilon) * gain + shift

def rotary(inputs):
    rows = inputs.shape[-2]
    shaped = inputs.reshape(inputs.shape[:-1] + (HEADS, HEAD))
    half = ROT // 2
    position = jnp.arange(rows, dtype=jnp.float32)
    inverse = rotary_base ** (-2.0 * jnp.arange(half, dtype=jnp.float32) / ROT)
    angle = position[:, None] * inverse[None, :]
    cosine = jnp.cos(angle)[:, None, :]
    sine = jnp.sin(angle)[:, None, :]
    first = shaped[..., :half]
    second = shaped[..., half:ROT]
    turned = jnp.concatenate([first * cosine - second * sine, second * cosine + first * sine, shaped[..., ROT:]], axis=-1)
    return turned.reshape(inputs.shape)

def unpack(small):
    extents = [D, D, D, D, D, D, 3 * D, D, FF, D]
    pieces = []
    offset = 0
    for extent in extents:
        pieces.append(small[offset:offset + extent])
        offset = offset + extent
    return pieces

def product(left, right):
    return jnp.einsum('gtd,de->gte', left, right, precision=lax.Precision.HIGHEST)

def rewards_of(params, token_rows, lengths):
    table, in_w, out_w, up_w, down_w, small, heads = params
    pieces = unpack(small)
    group, rows = token_rows.shape
    embedded = jnp.take(table, token_rows, axis=0)
    attn_in = low(layer_norm(embedded, pieces[0], pieces[1]))
    projected = low_back(product(attn_in, in_w) + pieces[6])
    queries = low(rotary(projected[..., :D])).reshape(group, rows, HEADS, HEAD)
    keys = low(rotary(projected[..., D:2 * D])).reshape(group, rows, HEADS, HEAD)
    values = low(projected[..., 2 * D:]).reshape(group, rows, HEADS, HEAD)
    raw = low_back(jnp.einsum('gqhd,gkhd->ghqk', queries, keys, precision=lax.Precision.HIGHEST))
    causal = jnp.arange(rows)[:, None] >= jnp.arange(rows)[None, :]
    scores = jnp.where(causal, raw * HEAD ** (-0.5), -jnp.inf)
    probs = low(jnp.exp(scores - jax.nn.logsumexp(scores, axis=-1, keepdims=True)))
    mixed = jnp.einsum('ghqk,gkhd->gqhd', probs, values, precision=lax.Precision.HIGHEST)
    context = low(low_back(mixed)).reshape(group, rows, D)
    attn_out = low_back(product(context, out_w) + pieces[7])
    mlp_in = low(layer_norm(embedded, pieces[2], pieces[3]))
    hidden_pre = low_back(product(mlp_in, up_w) + pieces[8])
    hidden = low(jax.nn.gelu(hidden_pre, approximate=False))
    mlp_out = low_back(product(hidden, down_w) + pieces[9])
    output = embedded + attn_out + mlp_out
    final = layer_norm(output, pieces[4], pieces[5])
    pick = jnp.arange(rows)[None, :] == (lengths - 1)[:, None]
    last = lax.optimization_barrier(jnp.sum(jnp.where(pick[..., None], final, 0.0), axis=1))
    return jnp.dot(last, heads, precision=lax.Precision.HIGHEST)

def group_loss(params, token_rows, lengths, margins, valid, pair_count):
    rewards = rewards_of(params, token_rows, lengths)
    gap = rewards[0::2] - rewards[1::2]
    hinge = jnp.maximum(margins[:, None] - gap, 0.0)
    return jnp.sum(valid[:, None] * hinge) / (K * pair_count)

def lamb(weight, first, second, grad):
    weight = weight.astype(jnp.float32)
    new_first = beta_first * first.astype(jnp.float32) + (1.0 - beta_first) * grad
    new_second = beta_second * second.astype(jnp.float32) + (1.0 - beta_second) * grad * grad
    update = new_first / (1.0 - beta_first ** STEP) / (jnp.sqrt(new_second / (1.0 - beta_second ** STEP)) + adam_epsilon) + weight_decay * weight
    weight_norm = jnp.sqrt(jnp.sum(weight * weight))
    update_norm = jnp.sqrt(jnp.sum(update * update))
    new_weight = weight - learn_rate * (weight_norm / update_norm) * update
    return (new_weight, new_first, new_second, weight_norm, update_norm)

def reference(token_ids, seq_lengths, pair_margins, pair_valid, embed_table, in_proj, out_proj, up_proj, down_proj, small_params, reward_heads, first_embed, first_in, first_out, first_up, first_down, first_small, first_heads, second_embed, second_in, second_out, second_up, second_down, second_small, second_heads):
    weights = (embed_table, in_proj, out_proj, up_proj, down_proj, small_params, reward_heads)
    params = tuple((item.astype(jnp.float32) for item in weights))
    pair_count = jnp.sum(pair_valid.astype(jnp.float32))
    group = min(SEQS, max(2, 4096 // LEN))
    blocks = SEQS // group
    token_blocks = token_ids.reshape(blocks, group, LEN)
    length_blocks = seq_lengths.reshape(blocks, group)
    margin_blocks = pair_margins.astype(jnp.float32).reshape(blocks, group // 2)
    valid_blocks = pair_valid.astype(jnp.float32).reshape(blocks, group // 2)

    def visit(carry, inputs):
        total, grads = carry
        token_rows, lengths, margins, valid = inputs
        value, pull = jax.vjp(lambda *weights_in: group_loss(weights_in, token_rows, lengths, margins, valid, pair_count), *params)
        parts = pull(jnp.ones_like(value))
        return ((total + value, tuple((left + right for left, right in zip(grads, parts)))), None)
    zeros = tuple((jnp.zeros_like(item) for item in params))
    (loss, grads), unused = lax.scan(visit, (jnp.zeros((), jnp.float32), zeros), (token_blocks, length_blocks, margin_blocks, valid_blocks))
    firsts = (first_embed, first_in, first_out, first_up, first_down, first_small, first_heads)
    seconds = (second_embed, second_in, second_out, second_up, second_down, second_small, second_heads)
    results = []
    weight_norms = []
    update_norms = []
    for index in range(7):
        new_weight, new_first, new_second, weight_norm, update_norm = lamb(weights[index], firsts[index], seconds[index], grads[index])
        results = results + [new_weight, new_first, new_second]
        weight_norms.append(weight_norm)
        update_norms.append(update_norm)
    norms = jnp.stack([jnp.stack(weight_norms), jnp.stack(update_norms)])
    return (loss, norms, results[0], results[1], results[2], results[3], results[4], results[5], results[6], results[7], results[8], results[9], results[10], results[11], results[12], results[13], results[14], results[15], results[16], results[17], results[18], results[19], results[20])
```

```python
import jax
import jax.numpy as jnp
import numpy as np
from jax import lax
from jax.experimental import pallas as pl
from jax.experimental.pallas import tpu as pltpu
from jax.sharding import PartitionSpec as P

D = 512
HEADS = 8
HEAD = 64
ROT = 16
FF = 2048
K = 8
STEP = 5
LEN = 128
SMALL = 7680
CHUNK = 512
HALF_IN = 3 * D // 2

norm_epsilon = 1e-05
beta_first = 0.9
beta_second = 0.999
adam_epsilon = 1e-06
weight_decay = 0.01
learn_rate = 0.3
rotary_base = 10000.0
first_scale = 1.0 / (1.0 - beta_first**STEP)
second_scale = 1.0 / (1.0 - beta_second**STEP)

f32 = jnp.float32
bf16 = jnp.bfloat16
exact = lax.Precision.HIGHEST
VMEM = pltpu.VMEM
SMEM = pltpu.SMEM
ANY = pl.ANY
G1, B1, G2, B2, GF, BF = [i * D for i in range(6)]
BIN = 6 * D
BOUT = BIN + 3 * D
BUP = BOUT + D
BDOWN = BUP + FF


def call(body, ins, outs, scratch=(), alias=None, work=(0, 0)):
    return pl.pallas_call(
        body,
        in_specs=[pl.BlockSpec(memory_space=space) for _, space in ins],
        out_specs=[pl.BlockSpec(memory_space=space) for _, _, space in outs],
        out_shape=[jax.ShapeDtypeStruct(shape, kind) for shape, kind, _ in outs],
        scratch_shapes=list(scratch),
        input_output_aliases=alias or {},
        cost_estimate=pl.CostEstimate(flops=work[0], bytes_accessed=work[1], transcendentals=0),
    )(*[array for array, _ in ins])


def dot(left, right, cl=1, cr=0, precision=None):
    return lax.dot_general(
        left, right, (((cl,), (cr,)), ((), ())), precision=precision, preferred_element_type=f32
    )


def iota(shape, axis):
    return lax.broadcasted_iota(jnp.int32, shape, axis)


def normed(value):
    center = value - jnp.mean(value, axis=-1, keepdims=True)
    spread = lax.rsqrt(jnp.mean(center * center, axis=-1, keepdims=True) + norm_epsilon)
    return center * spread, spread


def norm_back(unit, spread, grad):
    return spread * (
        grad
        - jnp.mean(grad, axis=-1, keepdims=True)
        - unit * jnp.mean(grad * unit, axis=-1, keepdims=True)
    )


def rotary_table():
    lane = np.arange(128)
    place = lane % HEAD
    half = ROT // 2
    inverse = rotary_base ** (-2.0 * (place % half) / ROT)
    angle = np.arange(LEN)[:, None] * inverse[None, :]
    turning = place < ROT
    cosine = np.where(turning, np.cos(angle), 1.0)
    early = np.where(place < half, -np.sin(angle), 0.0)
    late = np.where(turning & (place >= half), np.sin(angle), 0.0)
    return np.concatenate([cosine, early, late], axis=1).astype(np.float32)


def turns(places, table):
    pick = (iota((places.shape[0], LEN), 1).astype(f32) == places).astype(f32)
    rows = dot(pick, table, precision=exact)
    return [jnp.concatenate([rows[:, i : i + 128]] * 4, axis=1) for i in (0, 128, 256)]


def rotate(value, turn):
    return (
        value * turn[0]
        + pltpu.roll(value, D - 8, 1) * turn[1]
        + pltpu.roll(value, 8, 1) * turn[2]
    )


def rotate_back(value, turn):
    return (
        value * turn[0]
        - pltpu.roll(value, D - 8, 1) * turn[1]
        - pltpu.roll(value, 8, 1) * turn[2]
    )


def by_head(value, lanes):
    seqs = value.shape[0]
    head = iota((1, HEADS, D), 1)
    own = iota((1, HEADS, D), 2) // HEAD == head
    spread = jnp.where(own, value.reshape(seqs, 1, D), 0.0).reshape(seqs * HEADS, D)
    if lanes > seqs * HEADS:
        spread = jnp.concatenate([spread] * (lanes // (seqs * HEADS)), axis=0)
    return spread.astype(bf16)


def own_lanes(seqs, lanes):
    lane = iota((seqs, lanes), 1) % (seqs * HEADS)
    return lane // HEADS == iota((seqs, lanes), 0)


def to_lanes(column, lanes):
    seqs = column.shape[0]
    return jnp.sum(jnp.where(own_lanes(seqs, lanes), column, 0.0), axis=0, keepdims=True)


def head_sums(value, lanes):
    seqs = value.shape[0]
    member = (iota((D, lanes), 0) // HEAD == iota((D, lanes), 1) % HEADS).astype(f32)
    return jnp.sum(
        jnp.where(own_lanes(seqs, lanes), dot(value, member, precision=exact), 0.0),
        axis=0,
        keepdims=True,
    )


def head_spread(weights, seqs):
    lanes = weights.shape[1]
    first = iota((lanes, D), 0) < seqs * HEADS
    member = (first & (iota((lanes, D), 1) // HEAD == iota((lanes, D), 0) % HEADS)).astype(f32)
    return dot(weights, member, precision=exact)


def allowed(meta, seqs, lanes, first_seq, lengths):
    rows = meta.shape[0]
    lane = iota((rows, lanes), 1) % (seqs * HEADS)
    mine = (lane // HEADS + first_seq).astype(f32) == meta[:, 1:2]
    return mine & (meta[:, 2:3] < lengths) & (meta[:, 3:4] > 0.0)


def keys_values(tokens, meta, weights, small, table):
    unit, spread = normed(tokens.astype(f32))
    inputs = (unit * small[:, G1 : G1 + D] + small[:, B1 : B1 + D]).astype(bf16)
    both = dot(inputs, weights[:, D:]) + small[:, BIN + D : BIN + 3 * D]
    turn = turns(meta[:, 2:3], table)
    keys = rotate(both[:, :D], turn).astype(bf16)
    values = both[:, D:].astype(bf16)
    return unit, spread, inputs, keys, values, turn


def scores_of(keys, queries, mask):
    return jnp.where(mask, dot(keys, queries, 1, 1) * HEAD ** (-0.5), -1e30)


def updated(weight, first, second):
    return first * first_scale / (jnp.sqrt(second * second_scale) + adam_epsilon) + (
        weight_decay * weight
    )


def moments(weight, first, second, grad):
    new_first = beta_first * first + (1.0 - beta_first) * grad
    new_second = beta_second * second + (1.0 - beta_second) * grad * grad
    return new_first, new_second, updated(weight, new_first, new_second)


def total(value):
    return jnp.sum(jnp.sum(value, axis=1, keepdims=True), axis=0, keepdims=True)


def fetch(source, start, size, target, sem):
    copy = pltpu.make_async_copy(source.at[pl.ds(start, size)], target, sem)
    copy.start()
    return copy


def store(source, target, start, size, sem):
    copy = pltpu.make_async_copy(source, target.at[pl.ds(start, size)], sem)
    copy.start()
    return copy


def last_rows_body(seqs, rows, place_ref, table_ref, out_ref, buffer, sem):
    copies = []
    for s in range(seqs):
        place = place_ref[s]
        start = pl.multiple_of((jnp.clip(place, 0, rows - 8) // 8) * 8, 8)
        copy = pltpu.make_async_copy(table_ref.at[pl.ds(start, 8)], buffer.at[s], sem.at[s])
        copy.start()
        copies.append(copy)
    for s in range(seqs):
        copies[s].wait()
    picked = []
    for s in range(seqs):
        place = place_ref[s]
        start = (jnp.clip(place, 0, rows - 8) // 8) * 8
        inside = (place >= 0) & (place < rows)
        row = jnp.where(inside, place - start, -1)
        hit = iota((8, D), 0) == row
        picked.append(
            jnp.sum(jnp.where(hit, buffer[s].astype(f32), 0.0), axis=0, keepdims=True)
        )
    out_ref[...] = jnp.concatenate(picked, axis=0)


def collect_body(
    seqs,
    group,
    rows,
    local_ref,
    table_ref,
    tokens_ref,
    meta_ref,
    lanes_ref,
    count_ref,
    table,
    slots,
    tokens,
    meta,
    lanes,
    far,
    sem,
):
    load = pltpu.make_async_copy(table_ref, table, sem)
    load.start()
    local = local_ref[...]
    inside = (local >= 0) & (local < rows)
    mask = inside.astype(f32)
    before = (iota((LEN, LEN), 0) < iota((LEN, LEN), 1)).astype(bf16)
    in_row = dot(mask.astype(bf16), before)
    sums = jnp.sum(mask, axis=1, keepdims=True)
    above = (iota((seqs, seqs), 1) < iota((seqs, seqs), 0)).astype(f32)
    offset = dot(above, jnp.broadcast_to(sums, (seqs, LEN)), precision=exact)
    slots[...] = jnp.where(inside, in_row + offset, -1.0)
    owned = jnp.sum(mask).astype(jnp.int32)
    count_ref[0] = owned
    count_ref[1] = jnp.sum(mask[:group]).astype(jnp.int32)
    load.wait()

    def chunk(c, carry):
        slot = (iota((CHUNK, LEN), 0) + c * CHUNK).astype(f32)
        lane = iota((1, LEN), 1).astype(f32)

        def sequence(s, found):
            place, code = found
            hit = slots[pl.ds(s, 1), :] == slot
            row = local_ref[pl.ds(s, 1), :].astype(f32)
            tag = lane + (s * LEN + 1).astype(f32)
            return (place + jnp.where(hit, row, 0.0), code + jnp.where(hit, tag, 0.0))

        zero = jnp.zeros((CHUNK, LEN), f32)
        place, code = lax.fori_loop(0, seqs, sequence, (zero, zero))
        place = jnp.sum(place, axis=1, keepdims=True)
        code = jnp.sum(code, axis=1, keepdims=True)
        valid = code > 0.0
        place = jnp.where(valid, place, -1.0)
        code = jnp.maximum(code - 1.0, 0.0)
        sequence_at = jnp.floor(code * (1.0 / LEN))
        at = code - sequence_at * LEN
        same = iota((CHUNK, CHUNK), 0) == iota((CHUNK, CHUNK), 1)
        row = jnp.sum(jnp.where(same, place, 0.0), axis=0, keepdims=True)
        lanes[...] = jnp.broadcast_to(row, (8, CHUNK))
        earlier = (place == row) & (iota((CHUNK, CHUNK), 1) < iota((CHUNK, CHUNK), 0))
        seen = jnp.sum(earlier.astype(f32), axis=1, keepdims=True)

        def compare(o, found):
            pltpu.sync_copy(lanes_ref.at[pl.ds(pl.multiple_of(o * 8, 8), 8)], far)
            return found + jnp.sum((place == far[0:1, :]).astype(f32), axis=1, keepdims=True)

        seen = lax.fori_loop(0, c, compare, seen)
        opening = valid & (seen == 0.0)
        column = iota((CHUNK, LEN), 1)
        meta[...] = jnp.where(
            column == 0,
            place,
            jnp.where(
                column == 1,
                sequence_at,
                jnp.where(column == 2, at, jnp.where(column == 3, valid.astype(f32), jnp.where(column == 4, opening.astype(f32), 0.0))),
            ),
        )
        picked = jnp.zeros((CHUNK, D), f32)
        for start in range(0, rows, CHUNK):
            size = min(CHUNK, rows - start)
            hot = (iota((CHUNK, size), 1) + start).astype(f32) == place
            picked = picked + dot(hot.astype(f32).astype(bf16), table[start : start + size, :])
        tokens[...] = picked.astype(bf16)
        start = pl.multiple_of(c * CHUNK, CHUNK)
        first = pl.multiple_of(c * 8, 8)
        pltpu.sync_copy(tokens, tokens_ref.at[pl.ds(start, CHUNK)])
        pltpu.sync_copy(meta, meta_ref.at[pl.ds(start, CHUNK)])
        pltpu.sync_copy(lanes, lanes_ref.at[pl.ds(first, 8)])
        return carry

    lax.fori_loop(0, (owned + CHUNK - 1) // CHUNK, chunk, 0)


def decay_body(
    rows, block, weight_ref, first_ref, second_ref, first_out, second_out, update_out, sums_ref
):
    step = pl.program_id(0)
    weight = weight_ref[...].astype(f32)
    first = beta_first * first_ref[...].astype(f32)
    second = beta_second * second_ref[...].astype(f32)
    first_out[...] = first
    second_out[...] = second
    update = updated(weight, first, second)
    update_out[...] = update.astype(bf16)
    inside = iota((block, D), 0) + step * block < rows

    @pl.when(step == 0)
    def _():
        sums_ref[...] = jnp.zeros_like(sums_ref)

    square = jnp.where(inside, weight * weight, 0.0)
    sums_ref[0:8, :] += jnp.sum(square.reshape(block // 8, 8, D), axis=0)
    square = jnp.where(inside, update * update, 0.0)
    sums_ref[8:16, :] += jnp.sum(square.reshape(block // 8, 8, D), axis=0)


def decay(weight, first, second):
    rows = weight.shape[0]
    block = 1024
    spec = pl.BlockSpec((block, D), lambda i: (i, 0))
    return pl.pallas_call(
        lambda *refs: decay_body(rows, block, *refs),
        grid=(pl.cdiv(rows, block),),
        in_specs=[spec] * 3,
        out_specs=[spec] * 3 + [pl.BlockSpec((16, D), lambda i: (0, 0))],
        out_shape=[
            jax.ShapeDtypeStruct((rows, D), f32),
            jax.ShapeDtypeStruct((rows, D), f32),
            jax.ShapeDtypeStruct((rows, D), bf16),
            jax.ShapeDtypeStruct((16, D), f32),
        ],
        cost_estimate=pl.CostEstimate(
            flops=30 * rows * D, bytes_accessed=20 * rows * D, transcendentals=0
        ),
    )(weight, first, second)


def forward_body(
    wide,
    group,
    lanes,
    scal_ref,
    count_ref,
    mine_ref,
    other_ref,
    last_ref,
    up_ref,
    down_ref,
    small_ref,
    bias_ref,
    info_ref,
    table_ref,
    tokens_ref,
    meta_ref,
    send_ref,
    weights_ref,
    query_ref,
    pre_ref,
    embed_ref,
    keys_ref,
    values_ref,
    tokens,
    meta,
    keys,
    values,
    peak,
    mass,
    sem,
):
    depth = mine_ref.shape[1] - 16
    own = pl.multiple_of(scal_ref[0] * HALF_IN, 128)
    far = pl.multiple_of(HALF_IN - scal_ref[0] * HALF_IN, 128)
    for f in range(wide):
        weights_ref[f * depth : (f + 1) * depth, pl.ds(own, HALF_IN)] = mine_ref[f, :depth, :]
        weights_ref[f * depth : (f + 1) * depth, pl.ds(far, HALF_IN)] = other_ref[f, :depth, :]
    small = small_ref[...]
    table = table_ref[...]
    embedded = jnp.zeros((group, D), f32)
    for f in range(wide):
        embedded = embedded + last_ref[f, :group, :].astype(f32)
    embed_ref[...] = embedded
    unit, _ = normed(embedded)
    inputs = (unit * small[:, G1 : G1 + D] + small[:, B1 : B1 + D]).astype(bf16)
    wide_in = (unit * small[:, G2 : G2 + D] + small[:, B2 : B2 + D]).astype(bf16)
    length = info_ref[:group, 2:3]
    query = dot(inputs, weights_ref[:, :D]) + small[:, BIN : BIN + D]
    query = rotate(query, turns(length - 1.0, table)).astype(bf16).astype(f32)
    query_ref[...] = query
    pre = dot(wide_in, up_ref[...]) + bias_ref[...]
    pre_ref[...] = pre
    hidden, _ = gelu_parts(pre)
    mlp = dot(hidden.astype(bf16), down_ref[...])
    queries = by_head(query, lanes)
    lengths = to_lanes(length, lanes)
    peak[...] = jnp.full_like(peak, -1e30)
    mass[...] = jnp.zeros_like(mass)

    def chunk(c, carry):
        start = pl.multiple_of(c * CHUNK, CHUNK)
        one = fetch(tokens_ref, start, CHUNK, tokens, sem.at[0])
        two = fetch(meta_ref, start, CHUNK, meta, sem.at[1])
        one.wait()
        two.wait()
        _, _, _, key, value, _ = keys_values(
            tokens[...], meta[...], weights_ref[...], small, table
        )
        keys[...] = key
        values[...] = value
        one = store(keys, keys_ref, start, CHUNK, sem.at[0])
        two = store(values, values_ref, start, CHUNK, sem.at[1])
        mask = allowed(meta[...], group, lanes, 0, lengths)
        scores = scores_of(key, queries, mask)
        top = jnp.maximum(peak[...], jnp.max(scores, axis=0, keepdims=True))
        part = jnp.where(mask, jnp.exp(scores - top), 0.0)
        mass[...] = mass[...] * jnp.exp(peak[...] - top) + jnp.sum(part, axis=0, keepdims=True)
        peak[...] = top
        one.wait()
        two.wait()
        return carry

    lax.fori_loop(0, (count_ref[1] + CHUNK - 1) // CHUNK, chunk, 0)
    send = jnp.concatenate(
        [
            mlp,
            jnp.broadcast_to(peak[...], (group, lanes)),
            jnp.broadcast_to(mass[...], (group, lanes)),
        ],
        axis=1,
    )
    for f in range(wide):
        send_ref[f] = send


def mix_body(
    wide,
    group,
    lanes,
    count_ref,
    got_ref,
    query_ref,
    embed_ref,
    small_ref,
    info_ref,
    keys_ref,
    values_ref,
    meta_ref,
    send_ref,
    base_ref,
    total_ref,
    keys,
    values,
    meta,
    mixed,
    sem,
):
    small = small_ref[...]
    got = [got_ref[f] for f in range(wide)]
    peaks = [g[:1, D : D + lanes] for g in got]
    top = peaks[0]
    for f in range(1, wide):
        top = jnp.maximum(top, peaks[f])
    mass = jnp.zeros((1, lanes), f32)
    mlp = jnp.zeros((group, D), f32)
    for f in range(wide):
        mass = mass + jnp.exp(peaks[f] - top) * got[f][:1, D + lanes :]
        mlp = mlp + got[f][:, :D]
    log_total = top + jnp.log(mass)
    total_ref[...] = log_total
    base_ref[...] = embed_ref[...] + (mlp + small[:, BDOWN : BDOWN + D])
    queries = by_head(query_ref[...], lanes)
    lengths = to_lanes(info_ref[:group, 2:3], lanes)
    mixed[...] = jnp.zeros_like(mixed)

    def chunk(c, carry):
        start = pl.multiple_of(c * CHUNK, CHUNK)
        one = fetch(keys_ref, start, CHUNK, keys, sem.at[0])
        two = fetch(meta_ref, start, CHUNK, meta, sem.at[1])
        three = fetch(values_ref, start, CHUNK, values, sem.at[2])
        one.wait()
        two.wait()
        three.wait()
        mask = allowed(meta[...], group, lanes, 0, lengths)
        scores = scores_of(keys[...], queries, mask)
        probs = jnp.where(mask, jnp.exp(scores - log_total), 0.0).astype(bf16)
        mix = dot(probs, values[...], 0, 0)[: group * HEADS].reshape(group, HEADS, D)
        own_head = iota((1, HEADS, D), 2) // HEAD == iota((1, HEADS, D), 1)
        mixed[...] += jnp.sum(jnp.where(own_head, mix, 0.0), axis=1)
        return carry

    lax.fori_loop(0, (count_ref[1] + CHUNK - 1) // CHUNK, chunk, 0)
    for f in range(wide):
        send_ref[f] = mixed[...]


def gelu_parts(pre):
    chance = 0.5 * (1.0 + lax.erf(pre * (0.5**0.5)))
    density = jnp.exp(-0.5 * pre * pre) * ((2.0 * np.pi) ** -0.5)
    return pre * chance, chance + pre * density


def judged(output, small, heads, info):
    seqs = output.shape[0]
    unit, spread = normed(output)
    final = unit * small[:, GF : GF + D] + small[:, BF : BF + D]
    rewards = dot(final, heads, precision=exact)
    even = iota((seqs, 1), 0) % 2 == 0
    partner = jnp.where(
        even, pltpu.roll(rewards, seqs - 1, 0), pltpu.roll(rewards, 1, 0)
    )
    side = jnp.where(even, 1.0, -1.0)
    room = info[:, 0:1] - side * (rewards - partner)
    counted = iota((seqs, rewards.shape[1]), 1) < K
    hinge = jnp.where(counted, info[:, 1:2] * jnp.maximum(room, 0.0), 0.0)
    grad_rewards = jnp.where(counted & (room > 0.0), -side * info[:, 1:2], 0.0)
    grad_final = dot(grad_rewards, heads, 1, 1, precision=exact)
    grad_output = norm_back(unit, spread, grad_final * small[:, GF : GF + D])
    return unit, final, grad_rewards, grad_final, grad_output, jnp.where(even, hinge, 0.0)


def pack_rows(value, width):
    rows, columns = value.shape
    if columns <= width:
        if columns == width:
            return value
        return jnp.concatenate([value, jnp.zeros((rows, width - columns), f32)], axis=1)
    parts = columns // width
    return jnp.concatenate([value[:, i * width : (i + 1) * width] for i in range(parts)], axis=0)


def unpack_rows(value, rows, columns):
    width = value.shape[1]
    if columns <= width:
        return value[:rows, :columns]
    parts = columns // width
    return jnp.concatenate([value[i * rows : (i + 1) * rows] for i in range(parts)], axis=1)


def backward_body(
    wide,
    group,
    lanes,
    count_ref,
    got_ref,
    base_ref,
    total_ref,
    weights_ref,
    query_ref,
    pre_ref,
    embed_ref,
    up_ref,
    down_ref,
    out_ref,
    small_ref,
    heads_ref,
    info_ref,
    table_ref,
    tokens_ref,
    meta_ref,
    keys_ref,
    values_ref,
    send_ref,
    share_ref,
    tokens,
    meta,
    keys,
    values,
    turned,
    grad_query,
    sums,
    sem,
):
    small = small_ref[...]
    table = table_ref[...]
    length = info_ref[:group, 2:3]
    lengths = to_lanes(length, lanes)
    log_total = total_ref[...]
    context = got_ref[0]
    for f in range(1, wide):
        context = context + got_ref[f]
    context_low = context.astype(bf16)
    attn = dot(context_low, out_ref[...]) + small[:, BOUT : BOUT + D]
    output = base_ref[...] + attn
    _, _, _, _, grad_output, _ = judged(output, small, heads_ref[...], info_ref[:group])
    low = grad_output.astype(bf16)
    grad_context = dot(low, out_ref[...], 1, 1).astype(bf16).astype(f32)
    inner = head_sums(grad_context * context, lanes)
    grad_hidden = dot(low, down_ref[...], 1, 1)
    hidden, slope = gelu_parts(pre_ref[...])
    grad_pre = (grad_hidden * slope).astype(bf16)
    grad_wide = dot(grad_pre, up_ref[...], 1, 1)
    share_ref[...] = jnp.concatenate(
        [
            output,
            grad_context,
            query_ref[...],
            context_low.astype(f32),
            embed_ref[...],
            jnp.broadcast_to(log_total, (group, lanes)),
            jnp.broadcast_to(inner, (group, lanes)),
            hidden.astype(bf16).astype(f32),
        ],
        axis=1,
    )
    queries = by_head(query_ref[...], lanes)
    contexts = by_head(grad_context, lanes)
    turned[...] = jnp.zeros_like(turned)
    grad_query[...] = jnp.zeros_like(grad_query)
    sums[...] = jnp.zeros_like(sums)
    real = group * HEADS

    def chunk(c, carry):
        start = pl.multiple_of(c * CHUNK, CHUNK)
        one = fetch(tokens_ref, start, CHUNK, tokens, sem.at[0])
        two = fetch(meta_ref, start, CHUNK, meta, sem.at[1])
        three = fetch(keys_ref, start, CHUNK, keys, sem.at[2])
        four = fetch(values_ref, start, CHUNK, values, sem.at[3])
        one.wait()
        two.wait()
        three.wait()
        four.wait()
        weights = weights_ref[...]
        unit, _ = normed(tokens[...].astype(f32))
        inputs = (unit * small[:, G1 : G1 + D] + small[:, B1 : B1 + D]).astype(bf16)
        turn = turns(meta[:, 2:3], table)
        mask = allowed(meta[...], group, lanes, 0, lengths)
        probs, grads = attention_grads(
            keys[...], values[...], queries, contexts, mask, log_total, inner
        )
        lane = iota((1, lanes), 1)
        if lanes > real:
            both = jnp.where(lane < real, grads, probs).astype(bf16)
            grads_once = jnp.where(lane < real, grads, 0.0).astype(bf16)
            probs_once = jnp.where(lane < real, probs, 0.0).astype(bf16)
        else:
            grads_once = grads.astype(bf16)
            probs_once = probs.astype(bf16)
            both = jnp.concatenate([grads_once, probs_once], axis=1)
        grad_keys, grad_values, low_keys = key_grads(
            grads_once, probs_once, queries, contexts, turn
        )
        lane_from = iota((D, 128), 0)
        rot = (lane_from // HEAD == iota((D, 128), 1) // ROT) & (
            lane_from % HEAD == iota((D, 128), 1) % ROT
        )
        narrow = dot(low_keys, rot.astype(bf16)).astype(bf16)
        turned[...] += dot(inputs, jnp.concatenate([both, narrow], axis=1), 0, 0)
        mix = dot(grads_once, keys[...], 0, 0)[:real].reshape(group, HEADS, D)
        own_head = iota((1, HEADS, D), 2) // HEAD == iota((1, HEADS, D), 1)
        grad_query[...] += jnp.sum(jnp.where(own_head, mix, 0.0), axis=1)
        grad_inputs = dot(low_keys, weights[:, D : 2 * D], 1, 1) + dot(
            grad_values.astype(bf16), weights[:, 2 * D :], 1, 1
        )
        sums[0:1, :] += jnp.sum(grad_inputs * unit, axis=0, keepdims=True)
        sums[1:2, :] += jnp.sum(grad_inputs, axis=0, keepdims=True)
        sums[2:3, :] += jnp.sum(low_keys.astype(f32), axis=0, keepdims=True)
        sums[3:4, :] += jnp.sum(grad_values, axis=0, keepdims=True)
        return carry

    lax.fori_loop(0, (count_ref[1] + CHUNK - 1) // CHUNK, chunk, 0)
    back = rotate_back(grad_query[...], turns(length - 1.0, table))
    width = send_ref.shape[2]
    depth = D // wide
    tail = jnp.concatenate(
        [
            pack_rows(back, width),
            pack_rows(grad_wide, width),
            pack_rows(sums[...], width),
            pack_rows(grad_pre.astype(f32), width),
        ],
        axis=0,
    ).astype(bf16)
    for f in range(wide):
        send_ref[f, :depth, :] = turned[f * depth : (f + 1) * depth, :].astype(bf16)
        send_ref[f, depth:, :] = tail


def attention_grads(keys, values, queries, contexts, mask, log_total, inner):
    scores = scores_of(keys, queries, mask)
    probs = jnp.where(mask, jnp.exp(scores - log_total), 0.0)
    grad_probs = dot(values, contexts, 1, 1)
    grads = probs * (grad_probs - inner) * HEAD ** (-0.5)
    return probs, grads


def key_grads(grads_once, probs_once, queries, contexts, turn):
    grad_keys = rotate_back(dot(grads_once, queries), turn)
    grad_values = dot(probs_once, contexts)
    return grad_keys, grad_values.astype(bf16).astype(f32), grad_keys.astype(bf16)


def gather_body(wide, group, got_ref, send_ref):
    rows = got_ref.shape[1] - group
    folded = got_ref[0, :rows, :].astype(f32)
    for f in range(1, wide):
        folded = folded + got_ref[f, :rows, :].astype(f32)
    pieces = [got_ref[f, rows:, :].astype(f32) for f in range(wide)]
    send_ref[...] = jnp.concatenate([folded] + pieces, axis=0).astype(bf16)


def spread_body(parts, group, lanes, *refs):
    count_ref = refs[0]
    shares = refs[1 : 1 + parts]
    weights_ref, small_ref, info_ref, table_ref, tokens_ref, meta_ref = refs[
        1 + parts : 7 + parts
    ]
    grads_ref, tokens, meta, grads, sem = refs[7 + parts :]
    small = small_ref[...]
    table = table_ref[...]
    real = group * HEADS

    def chunk(c, carry):
        start = pl.multiple_of(c * CHUNK, CHUNK)
        one = fetch(tokens_ref, start, CHUNK, tokens, sem.at[0])
        two = fetch(meta_ref, start, CHUNK, meta, sem.at[1])
        one.wait()
        two.wait()
        weights = weights_ref[...]
        unit, spread, _, keys, values, turn = keys_values(
            tokens[...], meta[...], weights, small, table
        )
        raw_keys = jnp.zeros((CHUNK, D), f32)
        grad_values = jnp.zeros((CHUNK, D), f32)
        for part in range(parts):
            share = shares[part]
            lengths = to_lanes(info_ref[part * group : (part + 1) * group, 2:3], lanes)
            mask = allowed(meta[...], group, lanes, part * group, lengths)
            queries = by_head(share[:, 2 * D : 3 * D], lanes)
            contexts = by_head(share[:, D : 2 * D], lanes)
            probs, scored = attention_grads(
                keys,
                values,
                queries,
                contexts,
                mask,
                share[:1, 5 * D : 5 * D + lanes],
                share[:1, 5 * D + lanes : 5 * D + 2 * lanes],
            )
            if lanes > real:
                once = iota((1, lanes), 1) < real
                probs = jnp.where(once, probs, 0.0)
                scored = jnp.where(once, scored, 0.0)
            raw_keys = raw_keys + dot(scored.astype(bf16), queries)
            grad_values = grad_values + dot(probs.astype(bf16), contexts)
        low_keys = rotate_back(raw_keys, turn).astype(bf16)
        grad_inputs = dot(low_keys, weights[:, D : 2 * D], 1, 1) + dot(
            grad_values.astype(bf16), weights[:, 2 * D :], 1, 1
        )
        grads[...] = norm_back(unit, spread, grad_inputs * small[:, G1 : G1 + D])
        pltpu.sync_copy(grads, grads_ref.at[pl.ds(start, CHUNK)])
        return carry

    lax.fori_loop(0, (count_ref[0] + CHUNK - 1) // CHUNK, chunk, 0)


def place_scalars(values):
    lane = iota((1, 128), 1)
    row = jnp.zeros((1, 128), f32)
    for i, value in enumerate(values):
        row = row + jnp.where(lane == i, value, 0.0)
    return row


def owned_body(parts, wide, group, lanes, *refs):
    scal_ref = refs[0]
    shares = refs[1 : 1 + parts]
    folds = refs[1 + parts : 1 + 2 * parts]
    weights_ref, small_ref, heads_ref, info_ref, table_ref = refs[
        1 + 2 * parts : 6 + 2 * parts
    ]
    base = 6 + 2 * parts
    states = refs[base : base + 18]
    outs = refs[base + 18 :]
    state_outs = outs[:18]
    extra_ref, loss_ref, sums_ref = outs[18:21]
    small = small_ref[...]
    info = info_ref[...]
    hidden_width = FF // wide
    depth = D // wide
    real = group * HEADS
    seqs = parts * group
    joined = jnp.concatenate([shares[p][...] for p in range(parts)], axis=0)
    output = joined[:, :D]
    grad_context = joined[:, D : 2 * D].astype(bf16)
    context = joined[:, 3 * D : 4 * D].astype(bf16)
    embedded = joined[:, 4 * D : 5 * D]
    hidden = joined[:, 5 * D + 2 * lanes : 5 * D + 2 * lanes + hidden_width].astype(bf16)
    unit_out, final, grad_rewards, grad_final, grad_output, hinge = judged(
        output, small, heads_ref[...], info
    )
    loss_ref[...] = jnp.broadcast_to(total(hinge), (1, 128))
    low = grad_output.astype(bf16)
    unit, spread = normed(embedded)
    attn_in = (unit * small[:, G1 : G1 + D] + small[:, B1 : B1 + D]).astype(bf16)
    wide_in = (unit * small[:, G2 : G2 + D] + small[:, B2 : B2 + D]).astype(bf16)
    width = folds[0].shape[1]
    rows_d = group * max(1, D // width)
    rows_s = 8 * max(1, D // width)
    grad_query = []
    grad_wide = []
    sums = jnp.zeros((8, D), f32)
    grad_keys = jnp.zeros((depth, D), f32)
    grad_values = jnp.zeros((depth, D), f32)
    narrow = jnp.zeros((depth, 128), f32)
    grad_pre = [[] for f in range(wide)]
    for p in range(parts):
        fold = folds[p][...].astype(f32)
        at = depth
        grad_query.append(unpack_rows(fold[at : at + rows_d], group, D))
        at += rows_d
        grad_wide.append(unpack_rows(fold[at : at + rows_d], group, D))
        at += rows_d
        sums = sums + unpack_rows(fold[at : at + rows_s], 8, D)
        at += rows_s
        for f in range(wide):
            grad_pre[f].append(fold[at : at + group, :hidden_width])
            at += group
        queries = by_head(shares[p][:, 2 * D : 3 * D], real)
        contexts = by_head(shares[p][:, D : 2 * D], real)
        grad_keys = grad_keys + dot(fold[:depth, :real].astype(bf16), queries)
        grad_values = grad_values + dot(fold[:depth, real : 2 * real].astype(bf16), contexts)
        narrow = narrow + fold[:depth, 2 * real :]
    lane_to = iota((128, D), 1)
    rot = (lane_to // HEAD == iota((128, D), 0) // ROT) & (
        lane_to % HEAD == iota((128, D), 0) % ROT
    )
    turning = iota((1, D), 1) % HEAD < ROT
    grad_keys = jnp.where(turning, dot(narrow, rot.astype(f32), precision=exact), grad_keys)
    grad_query = jnp.concatenate(grad_query, axis=0).astype(bf16)
    grad_wide = jnp.concatenate(grad_wide, axis=0)
    pick = iota((depth, D), 1) == iota((depth, D), 0) + scal_ref[1] * depth
    pick = pick.astype(f32).astype(bf16)
    mine_in = dot(pick, attn_in, 1, 1).astype(bf16)
    mine_wide = dot(pick, wide_in, 1, 1).astype(bf16)
    mine_context = dot(pick, context, 1, 1).astype(bf16)
    grad_in = jnp.concatenate([dot(mine_in, grad_query), grad_keys, grad_values], axis=1)
    grad_out = dot(mine_context, low)
    grad_up = []
    bias_up = []
    for f in range(wide):
        piece = jnp.concatenate(grad_pre[f], axis=0)
        bias_up.append(jnp.sum(piece, axis=0, keepdims=True))
        grad_up.append(dot(mine_wide, piece.astype(bf16)))
    grad_up = jnp.concatenate(grad_up, axis=1)
    grad_down = dot(hidden, low, 0, 0)
    grad_first = dot(grad_query, weights_ref[:, :D], 1, 1)
    bias_low = jnp.sum(low.astype(f32), axis=0, keepdims=True)

    def column(value):
        return jnp.sum(value, axis=0, keepdims=True)

    grad_small = jnp.concatenate(
        [
            sums[0:1] + column(grad_first * unit),
            sums[1:2] + column(grad_first),
            column(grad_wide * unit),
            column(grad_wide),
            column(grad_final * unit_out),
            column(grad_final),
            column(grad_query.astype(f32)),
            sums[2:3],
            sums[3:4],
            bias_low,
        ]
        + bias_up
        + [bias_low],
        axis=1,
    )
    grad_heads = dot(final, grad_rewards, 0, 0, precision=exact)
    extra_ref[...] = (
        grad_output
        + norm_back(unit, spread, grad_first * small[:, G1 : G1 + D])
        + norm_back(unit, spread, grad_wide * small[:, G2 : G2 + D])
    )
    weight_sums = []
    update_sums = []
    for i, grad in enumerate([grad_in, grad_out, grad_up, grad_down, grad_small, grad_heads]):
        weight = states[3 * i][...].astype(f32)
        first, second, update = moments(
            weight, states[3 * i + 1][...].astype(f32), states[3 * i + 2][...].astype(f32), grad
        )
        state_outs[3 * i][...] = first
        state_outs[3 * i + 1][...] = second
        state_outs[3 * i + 2][...] = update
        weight_sums.append(total(weight * weight))
        update_sums.append(total(update * update))
    sums_ref[...] = place_scalars([0.0] + weight_sums + [0.0] + update_sums)


def touched_body(
    wide,
    lean,
    count_ref,
    place_ref,
    target_ref,
    extra_ref,
    sums_ref,
    decay_ref,
    info_ref,
    meta_ref,
    lanes_ref,
    tokens_ref,
    grads_ref,
    first_ref,
    second_ref,
    final_ref,
    first_out,
    second_out,
    update_out,
    send_ref,
    meta,
    meta_far,
    lanes,
    tokens,
    grads,
    grads_far,
    first,
    second,
    update,
    change,
    sem,
):
    count = count_ref[0]
    chunks = (count + CHUNK - 1) // CHUNK
    seqs = extra_ref.shape[0]
    change[...] = jnp.zeros_like(change)
    base = iota((CHUNK, seqs), 1).astype(f32)
    last = jnp.sum(
        jnp.where(
            iota((seqs, seqs), 0) == iota((seqs, seqs), 1), info_ref[:, 2:3] - 1.0, 0.0
        ),
        axis=0,
        keepdims=True,
    )

    def finish(c, carry):
        start = pl.multiple_of(c * CHUNK, CHUNK)
        one = fetch(meta_ref, start, CHUNK, meta, sem.at[0])
        two = fetch(grads_ref, start, CHUNK, grads, sem.at[1])
        one.wait()
        two.wait()
        at_last = (
            (meta[:, 1:2] == base) & (meta[:, 2:3] == last) & (meta[:, 3:4] > 0.0)
        ).astype(f32)
        grads[...] = grads[...] + dot(at_last, extra_ref[...], precision=exact)
        pltpu.sync_copy(grads, final_ref.at[pl.ds(start, CHUNK)])
        return carry

    lax.fori_loop(0, chunks, finish, 0)

    def rows(c, carry):
        start = pl.multiple_of(c * CHUNK, CHUNK)
        here = jnp.minimum(CHUNK, count - c * CHUNK)

        def ask(i, inner):
            place = place_ref[c * CHUNK + i]
            pltpu.make_async_copy(
                first_ref.at[pl.ds(place, 1)], first.at[pl.ds(i, 1)], sem.at[2]
            ).start()
            pltpu.make_async_copy(
                second_ref.at[pl.ds(place, 1)], second.at[pl.ds(i, 1)], sem.at[3]
            ).start()
            return inner

        lax.fori_loop(0, here, ask, 0)
        one = fetch(meta_ref, start, CHUNK, meta, sem.at[0])
        two = fetch(tokens_ref, start, CHUNK, tokens, sem.at[1])
        one.wait()
        two.wait()

        def gather(o, grad):
            far = pl.multiple_of(o * CHUNK, CHUNK)
            three = fetch(lanes_ref, pl.multiple_of(o * 8, 8), 8, lanes, sem.at[0])
            four = fetch(final_ref, far, CHUNK, grads_far, sem.at[1])
            three.wait()
            four.wait()
            same = ((meta[:, 0:1] == lanes[0:1, :]) & (meta[:, 3:4] > 0.0)).astype(f32)
            value = grads_far[...]
            slot = iota((CHUNK, 1), 0) + o * CHUNK
            value = jnp.where(slot < count, value, 0.0)
            high = value.astype(bf16)
            low = (value - high.astype(f32)).astype(bf16)
            pairs = same.astype(bf16)
            return grad + dot(pairs, high) + dot(pairs, low)

        grad = lax.fori_loop(0, chunks, gather, jnp.zeros((CHUNK, D), f32))

        def answer(i, inner):
            pltpu.make_async_copy(
                first_ref.at[pl.ds(0, 1)], first.at[pl.ds(0, 1)], sem.at[2]
            ).wait()
            pltpu.make_async_copy(
                second_ref.at[pl.ds(0, 1)], second.at[pl.ds(0, 1)], sem.at[3]
            ).wait()
            return inner

        lax.fori_loop(0, here, answer, 0)
        valid = meta[:, 3:4] > 0.0
        weight = tokens[...].astype(f32)
        old_first = jnp.where(valid, first[...], 0.0)
        old_second = jnp.where(valid, second[...], 1.0)
        new_first = old_first + (1.0 - beta_first) * grad
        new_second = old_second + (1.0 - beta_second) * grad * grad
        old = updated(weight, old_first, old_second)
        new = updated(weight, new_first, new_second)
        moved = jnp.where(meta[:, 4:5] > 0.0, new * new - old * old, 0.0)
        change[...] += jnp.sum(moved.reshape(CHUNK // 8, 8, D), axis=0)
        first[...] = new_first
        second[...] = new_second
        update[...] = new.astype(bf16)
        pltpu.sync_copy(update, update_out.at[pl.ds(start, CHUNK)])
        if lean:

            def put(i, inner):
                target = target_ref[c * CHUNK + i]

                @pl.when(target >= 0)
                def _():
                    pltpu.sync_copy(first.at[pl.ds(i, 1)], first_out.at[pl.ds(target, 1)])
                    pltpu.sync_copy(second.at[pl.ds(i, 1)], second_out.at[pl.ds(target, 1)])

                return inner

            lax.fori_loop(0, here, put, 0)
        else:
            pltpu.sync_copy(first, first_out.at[pl.ds(start, CHUNK)])
            pltpu.sync_copy(second, second_out.at[pl.ds(start, CHUNK)])
        return carry

    lax.fori_loop(0, chunks, rows, 0)
    weight_sum = total(decay_ref[0:8, :])
    update_sum = total(decay_ref[8:16, :]) + total(change[...])
    lane = iota((1, 128), 1)
    row = sums_ref[...] + jnp.where(lane == 0, weight_sum, 0.0)
    row = row + jnp.where(lane == 7, update_sum, 0.0)
    for f in range(wide):
        send_ref[f] = row


def scatter_body(
    count_ref, place_ref, first_ref, second_ref, one_ref, two_ref, one_out, two_out, one, two, sem
):
    count = count_ref[0]

    def rows(c, carry):
        start = pl.multiple_of(c * CHUNK, CHUNK)
        a = fetch(first_ref, start, CHUNK, one, sem.at[0])
        b = fetch(second_ref, start, CHUNK, two, sem.at[1])
        a.wait()
        b.wait()
        here = jnp.minimum(CHUNK, count - c * CHUNK)

        def put(i, inner):
            place = place_ref[c * CHUNK + i]

            @pl.when(place >= 0)
            def _():
                pltpu.make_async_copy(
                    one.at[pl.ds(i, 1)], one_out.at[pl.ds(place, 1)], sem.at[2]
                ).start()
                pltpu.make_async_copy(
                    two.at[pl.ds(i, 1)], two_out.at[pl.ds(place, 1)], sem.at[3]
                ).start()

            return inner

        def done(i, inner):
            @pl.when(place_ref[c * CHUNK + i] >= 0)
            def _():
                pltpu.make_async_copy(
                    one.at[pl.ds(0, 1)], one_out.at[pl.ds(0, 1)], sem.at[2]
                ).wait()
                pltpu.make_async_copy(
                    two.at[pl.ds(0, 1)], two_out.at[pl.ds(0, 1)], sem.at[3]
                ).wait()

            return inner

        lax.fori_loop(0, here, put, 0)
        lax.fori_loop(0, here, done, 0)
        return carry

    lax.fori_loop(0, (count + CHUNK - 1) // CHUNK, rows, 0)


def norms_of(got_ref, local):
    folded = got_ref[0]
    for f in range(1, got_ref.shape[0]):
        folded = folded + got_ref[f]
    lane = iota((1, 128), 1) % 7
    return jnp.sqrt(jnp.where(lane < 5, folded, local))


def lane_of(row, i):
    return jnp.sum(jnp.where(iota(row.shape, 1) == i, row, 0.0), axis=1, keepdims=True)


def apply_body(got_ref, local_ref, weight_ref, update_ref, *refs):
    smalls = refs[:12]
    out_ref, norms_ref = refs[12:14]
    small_outs = refs[14:]
    norms = norms_of(got_ref, local_ref[...])
    ratio = learn_rate * lane_of(norms, 0) / lane_of(norms, 7)
    out_ref[...] = weight_ref[...].astype(f32) - ratio * update_ref[...].astype(f32)

    @pl.when(pl.program_id(0) == 0)
    def _():
        norms_ref[...] = jnp.broadcast_to(norms, norms_ref.shape)
        for i in range(6):
            rate = learn_rate * lane_of(norms, i + 1) / lane_of(norms, i + 8)
            small_outs[i][...] = (
                smalls[2 * i][...].astype(f32) - rate * smalls[2 * i + 1][...]
            )


def apply(got, local, weight, update, smalls):
    rows = weight.shape[0]
    block = 1024
    spec = pl.BlockSpec((block, D), lambda i: (i, 0))

    def fixed(shape):
        return pl.BlockSpec(shape, lambda i: (0,) * len(shape))

    shapes = [smalls[2 * i].shape for i in range(6)]
    return pl.pallas_call(
        apply_body,
        grid=(pl.cdiv(rows, block),),
        in_specs=[fixed(got.shape), fixed(local.shape), spec, spec]
        + [fixed(item.shape) for item in smalls],
        out_specs=[spec, fixed((8, 128))] + [fixed(shape) for shape in shapes],
        out_shape=[jax.ShapeDtypeStruct((rows, D), f32), jax.ShapeDtypeStruct((8, 128), f32)]
        + [jax.ShapeDtypeStruct(shape, f32) for shape in shapes],
    )(got, local, weight, update, *smalls)


def patch_body(
    count_ref,
    place_ref,
    norms_ref,
    tokens_ref,
    update_ref,
    new_ref,
    new_out,
    tokens,
    update,
    rows,
    sem,
):
    count = count_ref[0]
    norms = norms_ref[0:1, :]
    ratio = learn_rate * lane_of(norms, 0) / lane_of(norms, 7)

    def chunk(c, carry):
        start = pl.multiple_of(c * CHUNK, CHUNK)
        a = fetch(tokens_ref, start, CHUNK, tokens, sem.at[0])
        b = fetch(update_ref, start, CHUNK, update, sem.at[1])
        a.wait()
        b.wait()
        rows[...] = tokens[...].astype(f32) - ratio * update[...].astype(f32)
        here = jnp.minimum(CHUNK, count - c * CHUNK)

        def put(i, inner):
            place = place_ref[c * CHUNK + i]

            @pl.when(place >= 0)
            def _():
                pltpu.make_async_copy(
                    rows.at[pl.ds(i, 1)], new_out.at[pl.ds(place, 1)], sem.at[2]
                ).start()

            return inner

        def done(i, inner):
            @pl.when(place_ref[c * CHUNK + i] >= 0)
            def _():
                pltpu.make_async_copy(
                    rows.at[pl.ds(0, 1)], new_out.at[pl.ds(0, 1)], sem.at[2]
                ).wait()

            return inner

        lax.fori_loop(0, here, put, 0)
        lax.fori_loop(0, here, done, 0)
        return carry

    lax.fori_loop(0, (count + CHUNK - 1) // CHUNK, chunk, 0)


def per_device(
    token_ids,
    seq_lengths,
    pair_margins,
    pair_valid,
    embed_table,
    in_proj,
    out_proj,
    up_proj,
    down_proj,
    small_params,
    reward_heads,
    first_embed,
    first_in,
    first_out,
    first_up,
    first_down,
    first_small,
    first_heads,
    second_embed,
    second_in,
    second_out,
    second_up,
    second_down,
    second_small,
    second_heads,
):
    wide = lax.axis_size("fsdp")
    parts = lax.axis_size("dp")
    group = wide
    seqs = parts * group
    dp = lax.axis_index("dp")
    own = lax.axis_index("fsdp")
    core = dp % 2
    depth = D // wide
    hidden_width = FF // wide
    rows = embed_table.shape[0]
    capacity = seqs * LEN
    lanes = max(128, group * HEADS)
    dma = pltpu.SemaphoreType.DMA

    def across(value, bit):
        return lax.ppermute(value, "dp", [(i, i ^ bit) for i in range(parts)])

    def everywhere(value):
        have = [value]
        bit = 1
        while bit < parts:
            have = have + [across(item, bit) for item in have]
            bit = bit * 2
        return have

    def exchanged(value):
        return lax.all_to_all(value, "fsdp", 0, 0, tiled=True)

    small = small_params.astype(f32).reshape(1, SMALL)
    heads = jnp.pad(reward_heads.astype(f32), ((0, 0), (0, 128 - K)))
    table = jnp.asarray(rotary_table())
    bias_up = lax.dynamic_slice(small, (0, BUP + own * hidden_width), (1, hidden_width))
    scal = jnp.stack([core, own]).astype(jnp.int32)
    slot = dp ^ jnp.arange(parts)
    valid = pair_valid.astype(f32)
    scale = valid / (K * jnp.sum(valid))
    margins = pair_margins.astype(f32).reshape(parts, group // 2)[slot]
    scale = scale.reshape(parts, group // 2)[slot]

    half = jnp.where(core == 0, in_proj[:, :HALF_IN], in_proj[:, HALF_IN:])
    high = token_ids // 256
    low = token_ids - high * 256
    label = jnp.concatenate(
        [high, low, jnp.broadcast_to(seq_lengths[:, None], (1, HALF_IN - 2 * LEN))], axis=1
    ).astype(bf16)
    label = jnp.broadcast_to(label, (16, HALF_IN))
    first_send = jnp.concatenate([half, label], axis=0)
    mine = exchanged(jnp.broadcast_to(first_send[None], (wide,) + first_send.shape))
    decayed = decay(embed_table, first_embed, second_embed)
    other = across(mine, 1)
    labels = [mine[:, depth, :], other[:, depth, :]]
    bit = 2
    while bit < parts:
        labels = labels + [across(item, bit) for item in labels]
        bit = bit * 2
    labels = jnp.concatenate(labels, axis=0).astype(f32)
    ids = labels[:, :LEN] * 256.0 + labels[:, LEN : 2 * LEN]
    local = ids.astype(jnp.int32) - own * rows
    length = labels[:, 2 * LEN : 2 * LEN + 1]
    info = jnp.concatenate(
        [
            jnp.repeat(margins.reshape(-1), 2)[:, None],
            jnp.repeat(scale.reshape(-1), 2)[:, None],
            length,
            jnp.zeros((seqs, 125), f32),
        ],
        axis=1,
    )
    group_ids = mine[:, depth, :].astype(f32)
    group_local = (
        group_ids[:, :LEN] * 256.0 + group_ids[:, LEN : 2 * LEN]
    ).astype(jnp.int32) - own * rows
    at_last = jnp.arange(LEN)[None, :] == (group_ids[:, 2 * LEN :][:, :1] - 1.0)
    last_place = jnp.sum(jnp.where(at_last, group_local, 0), axis=1)
    (last_rows,) = call(
        lambda *refs: last_rows_body(group, rows, *refs),
        [(last_place, SMEM), (embed_table, ANY)],
        [((group, D), f32, VMEM)],
        [VMEM((group, 8, D), bf16), dma((group,))],
    )

    narrow = depth * hidden_width // D
    up_send = up_proj.reshape(depth, wide, hidden_width).transpose(1, 0, 2)
    up_send = up_send.reshape(wide, narrow, D)
    half = jnp.where(core == 0, out_proj[:, : D // 2], out_proj[:, D // 2 :])
    half = half.reshape(depth // 2, D)
    second_send = jnp.concatenate(
        [
            jnp.broadcast_to(last_rows.astype(bf16)[None], (wide, group, D)),
            up_send,
            jnp.broadcast_to(half[None], (wide, depth // 2, D)),
        ],
        axis=1,
    )
    got = exchanged(second_send)
    tokens, meta, place_lanes, count = call(
        lambda *refs: collect_body(seqs, group, rows, *refs),
        [(local, VMEM), (embed_table, ANY)],
        [
            ((capacity, D), bf16, ANY),
            ((capacity, 128), f32, ANY),
            ((capacity // CHUNK * 8, CHUNK), f32, ANY),
            ((2,), jnp.int32, SMEM),
        ],
        [
            VMEM((rows, D), bf16),
            VMEM((seqs, LEN), f32),
            VMEM((CHUNK, D), bf16),
            VMEM((CHUNK, 128), f32),
            VMEM((8, CHUNK), f32),
            VMEM((8, CHUNK), f32),
            dma,
        ],
        work=(2 * CHUNK * rows * D, 2 * rows * D),
    )
    place = meta[:, 0].astype(jnp.int32)
    target = jnp.where(meta[:, 4] > 0.0, place, -1)
    up_columns = got[:, group : group + narrow].reshape(D, hidden_width)
    out_half = got[:, group + narrow :].reshape(D, D // 2)
    out_far = across(out_half, 1)
    out_full = jnp.concatenate(
        [jnp.where(core == 0, out_half, out_far), jnp.where(core == 0, out_far, out_half)], axis=1
    )

    wide_send = D + 2 * lanes
    send, weights, query, pre, embedded, keys, values = call(
        lambda *refs: forward_body(wide, group, lanes, *refs),
        [
            (scal, SMEM),
            (count, SMEM),
            (mine, VMEM),
            (other, VMEM),
            (got, VMEM),
            (up_columns, VMEM),
            (down_proj, VMEM),
            (small, VMEM),
            (bias_up, VMEM),
            (info, VMEM),
            (table, VMEM),
            (tokens, ANY),
            (meta, ANY),
        ],
        [
            ((wide, group, wide_send), f32, VMEM),
            ((D, 3 * D), bf16, VMEM),
            ((group, D), f32, VMEM),
            ((group, hidden_width), f32, VMEM),
            ((group, D), f32, VMEM),
            ((capacity, D), bf16, ANY),
            ((capacity, D), bf16, ANY),
        ],
        [
            VMEM((CHUNK, D), bf16),
            VMEM((CHUNK, 128), f32),
            VMEM((CHUNK, D), bf16),
            VMEM((CHUNK, D), bf16),
            VMEM((1, lanes), f32),
            VMEM((1, lanes), f32),
            dma((2,)),
        ],
        work=(2 * CHUNK * D * 3 * D, 8 * D * D),
    )
    got = exchanged(send)
    send, base, log_total = call(
        lambda *refs: mix_body(wide, group, lanes, *refs),
        [
            (count, SMEM),
            (got, VMEM),
            (query, VMEM),
            (embedded, VMEM),
            (small, VMEM),
            (info, VMEM),
            (keys, ANY),
            (values, ANY),
            (meta, ANY),
        ],
        [
            ((wide, group, D), f32, VMEM),
            ((group, D), f32, VMEM),
            ((1, lanes), f32, VMEM),
        ],
        [
            VMEM((CHUNK, D), bf16),
            VMEM((CHUNK, D), bf16),
            VMEM((CHUNK, 128), f32),
            VMEM((group, D), f32),
            dma((3,)),
        ],
        work=(2 * CHUNK * D * D, 4 * D * D),
    )
    got = exchanged(send)

    width = 2 * group * HEADS + 128
    split = max(1, D // width)
    tail = 2 * group * split + 8 * split
    send, share = call(
        lambda *refs: backward_body(wide, group, lanes, *refs),
        [
            (count, SMEM),
            (got, VMEM),
            (base, VMEM),
            (log_total, VMEM),
            (weights, VMEM),
            (query, VMEM),
            (pre, VMEM),
            (embedded, VMEM),
            (up_columns, VMEM),
            (down_proj, VMEM),
            (out_full, VMEM),
            (small, VMEM),
            (heads, VMEM),
            (info, VMEM),
            (table, VMEM),
            (tokens, ANY),
            (meta, ANY),
            (keys, ANY),
            (values, ANY),
        ],
        [
            ((wide, depth + tail + group, width), bf16, VMEM),
            ((group, 5 * D + 2 * lanes + hidden_width), f32, VMEM),
        ],
        [
            VMEM((CHUNK, D), bf16),
            VMEM((CHUNK, 128), f32),
            VMEM((CHUNK, D), bf16),
            VMEM((CHUNK, D), bf16),
            VMEM((D, width), f32),
            VMEM((group, D), f32),
            VMEM((8, D), f32),
            dma((4,)),
        ],
        work=(2 * CHUNK * D * 6 * D, 8 * D * D),
    )
    got = exchanged(send)
    shares = everywhere(share)
    (grads,) = call(
        lambda *refs: spread_body(parts, group, lanes, *refs),
        [(count, SMEM)]
        + [(item, VMEM) for item in shares]
        + [
            (weights, VMEM),
            (small, VMEM),
            (info, VMEM),
            (table, VMEM),
            (tokens, ANY),
            (meta, ANY),
        ],
        [((capacity, D), f32, ANY)],
        [VMEM((CHUNK, D), bf16), VMEM((CHUNK, 128), f32), VMEM((CHUNK, D), f32), dma((2,))],
        work=(2 * CHUNK * D * 8 * D, 8 * D * D),
    )
    (fold,) = call(
        lambda *refs: gather_body(wide, group, *refs),
        [(got, VMEM)],
        [((depth + tail + wide * group, width), bf16, VMEM)],
    )
    folds = everywhere(fold)
    states = [
        in_proj,
        first_in,
        second_in,
        out_proj,
        first_out,
        second_out,
        up_proj,
        first_up,
        second_up,
        down_proj,
        first_down,
        second_down,
        small_params.reshape(1, SMALL),
        first_small.reshape(1, SMALL),
        second_small.reshape(1, SMALL),
    ] + [
        jnp.pad(item, ((0, 0), (0, 128 - K))) for item in (reward_heads, first_heads, second_heads)
    ]
    results = call(
        lambda *refs: owned_body(parts, wide, group, lanes, *refs),
        [(scal, SMEM)]
        + [(item, VMEM) for item in shares]
        + [(item, VMEM) for item in folds]
        + [(item, VMEM) for item in (weights, small, heads, info, table)]
        + [(item, VMEM) for item in states],
        [(states[i // 3 * 3].shape, f32, VMEM) for i in range(18)]
        + [((seqs, D), f32, VMEM), ((1, 128), f32, VMEM), ((1, 128), f32, VMEM)],
    )
    moved = results[:18]
    extra, loss, sums = results[18:]
    lean = capacity > 8192
    keep = (rows, D) if lean else (capacity, D)
    _, row_first, row_second, row_update, send = call(
        lambda *refs: touched_body(wide, lean, *refs),
        [
            (count, SMEM),
            (place, SMEM),
            (target, SMEM),
            (extra, VMEM),
            (sums, VMEM),
            (decayed[3], VMEM),
            (info, VMEM),
            (meta, ANY),
            (place_lanes, ANY),
            (tokens, ANY),
            (grads, ANY),
            (decayed[0], ANY),
            (decayed[1], ANY),
        ],
        [
            ((capacity, D), f32, ANY),
            (keep, f32, ANY),
            (keep, f32, ANY),
            ((capacity, D), bf16, ANY),
            ((wide, 1, 128), f32, VMEM),
        ],
        [
            VMEM((CHUNK, 128), f32),
            VMEM((CHUNK, 128), f32),
            VMEM((8, CHUNK), f32),
            VMEM((CHUNK, D), bf16),
            VMEM((CHUNK, D), f32),
            VMEM((CHUNK, D), f32),
            VMEM((CHUNK, D), f32),
            VMEM((CHUNK, D), f32),
            VMEM((CHUNK, D), bf16),
            VMEM((8, D), f32),
            dma((4,)),
        ],
        alias={10: 0, 11: 1, 12: 2} if lean else {10: 0},
    )

    got = exchanged(send)
    embed_first, embed_second = (row_first, row_second) if lean else call(
        scatter_body,
        [
            (count, SMEM),
            (target, SMEM),
            (row_first, ANY),
            (row_second, ANY),
            (decayed[0], ANY),
            (decayed[1], ANY),
        ],
        [((rows, D), f32, ANY)] * 2,
        [VMEM((CHUNK, D), f32), VMEM((CHUNK, D), f32), dma((4,))],
        alias={4: 0, 5: 1},
        work=(0, 8 * CHUNK * D),
    )
    smalls = []
    for i in range(6):
        smalls = smalls + [states[3 * i], moved[3 * i + 2]]
    applied = apply(got, sums, embed_table, decayed[2], smalls)
    dense, norms = applied[:2]
    fresh = applied[2:]
    (embed_new,) = call(
        patch_body,
        [
            (count, SMEM),
            (target, SMEM),
            (norms, VMEM),
            (tokens, ANY),
            (row_update, ANY),
            (dense, ANY),
        ],
        [((rows, D), f32, ANY)],
        [VMEM((CHUNK, D), bf16), VMEM((CHUNK, D), bf16), VMEM((CHUNK, D), f32), dma((3,))],
        alias={5: 0},
    )
    outputs = [embed_new, embed_first, embed_second]
    for i in range(4):
        outputs = outputs + [fresh[i], moved[3 * i], moved[3 * i + 1]]
    outputs = outputs + [item.reshape(SMALL) for item in (fresh[4], moved[12], moved[13])]
    outputs = outputs + [item[:, :K] for item in (fresh[5], moved[15], moved[16])]
    return (loss[0, 0], norms[0, :14].reshape(2, 7)) + tuple(outputs)


def solution(mesh):
    sharded = P("fsdp", None)
    state = (sharded,) * 5 + (P(), P())
    return jax.shard_map(
        per_device,
        mesh=mesh,
        in_specs=(P(("dp", "fsdp"), None), P(("dp", "fsdp")), P(), P()) + state * 3,
        out_specs=(P(), P()) + (sharded,) * 15 + (P(),) * 6,
        check_vma=False,
    )
```
